32 devices in a mesh: row: 16 (over z, y, core), col: 2 (over x).
Axes of the slice: x: 2, y: 2, z: 4, core: 2. Of those that a mesh axis runs over, the one named last changes fastest.
Arguments:
- block_input: bfloat16 [25216, 768], P(('row', 'col')), may hold values from -60 to 60
- attention_in: bfloat16 [768, 2304], P('row', 'col'), may hold values from -0.21875 to 0.21875
- attention_out: bfloat16 [768, 768], P('row', 'col'), may hold values from -0.875 to 0.875
- expert_up: bfloat16 [16, 768, 3072], P('row', 'col'), may hold values from -0.21875 to 0.21875
- expert_down: bfloat16 [16, 3072, 768], P('row', None, 'col'), may hold values from -4 to 4
- router_weight: float32 [768, 16], replicated, may hold values from -0.109375 to 0.109375
- gain_attention: float32 [768], replicated, may hold values from 0.25 to 1.75
- gain_experts: float32 [768], replicated, may hold values from 0.25 to 1.75
- expert_ids: int32 [25216, 2], P(('row', 'col')), may hold values from 0 to 15, as said below
- expert_slots: int32 [25216, 2], P(('row', 'col')), may hold values from 0 to 135, as said below
- expert_capacity: int32 [16], replicated, may hold values from 68 to 136, as said below
- keep_mask: int32 [25216, 2], P(('row', 'col')), may hold values from 0 to 1
- output_grad: bfloat16 [25216, 768], P(('row', 'col')), may hold values from -6 to 6
Outputs:
- block_output: bfloat16 [25216, 768], P(('row', 'col'))
- input_grad: bfloat16 [25216, 768], P(('row', 'col'))
- attention_in_grad: float32 [768, 2304], P('row', 'col')
- attention_out_grad: float32 [768, 768], P('row', 'col')
- expert_up_grad: float32 [16, 768, 3072], P('row', 'col')
- expert_down_grad: float32 [16, 3072, 768], P('row', None, 'col')
- router_grad: float32 [768, 16], replicated
- gain_attention_grad: float32 [768], replicated
- gain_experts_grad: float32 [768], replicated
- residual_rms: float32 [3], replicated
The draws below stay inside these ranges and needn't reach their ends.
Inputs may be any that keep to these rules, and one draw needn't show every extreme that they name: `expert_ids`: each row names two different experts. In each aligned block of 788 rows (the rows of one device) no expert is named more than 136 times and one expert is named exactly 136 times; blocks on the same index of col share that expert. `expert_slots`: within one aligned block of 788 rows, the n pairs that name one expert carry the slots 0 to n - 1, each once. `expert_capacity`: the expert named 136 times in the blocks of col index 0 accepts 136 slots.
All inputs are finite; a program needn't handle non-finite values.
Results may differ from the reference program's by a relative error of at most 0.019.
Values may be sent and summed in bfloat16 or wider, within the bound.
A program may use at most 192 MiB of HBM per device.

```python
import math
import jax
import jax.numpy as jnp
from jax import lax

D = 768
HEADS = 12
HEAD_DIM = 64
FF = 3072
SEQ = 197
IMG_DEV = 4
TOK_DEV = 788
TOKENS = 25216
IMAGES = 128
EXPERTS = 16
CAP = 136
N_COL = 2


def hot_expert(base_key, column):
    return jax.random.randint(jax.random.fold_in(jax.random.fold_in(base_key, 17), column), (), 0, EXPERTS).astype(jnp.int32)


def route_table(base_key):
    blocks = TOKENS // TOK_DEV
    pairs = 2 * TOK_DEV
    rest = pairs - CAP
    weights = jax.random.randint(jax.random.fold_in(base_key, 11), (EXPERTS,), 4, 6).astype(jnp.int32)
    experts_iota = jnp.arange(EXPERTS, dtype=jnp.int32)
    position = jnp.arange(pairs, dtype=jnp.int32)

    def one_block(block_index):
        block_key = jax.random.fold_in(jax.random.fold_in(base_key, 13), block_index)
        hot = hot_expert(base_key, block_index % N_COL)
        others = jnp.where(experts_iota == hot, 0, weights)
        base_counts = rest * others // jnp.sum(others)
        leftover = rest - jnp.sum(base_counts)
        priority = jax.random.permutation(jax.random.fold_in(block_key, 1), EXPERTS).astype(jnp.int32)
        hot_priority = jnp.sum(jnp.where(experts_iota == hot, priority, 0))
        ranking = priority - (priority > hot_priority).astype(jnp.int32)
        extra = ((ranking < leftover) & (experts_iota != hot)).astype(jnp.int32)
        counts = jnp.where(experts_iota == hot, CAP, base_counts + extra)
        ends = jnp.cumsum(counts)
        starts = ends - counts
        labels = jnp.sum((ends[None, :] <= position[:, None]).astype(jnp.int32), axis=1)
        slot_values = position - jnp.take(starts, labels)
        order = jax.random.permutation(jax.random.fold_in(block_key, 2), TOK_DEV).astype(jnp.int32)
        ids_sorted = jnp.stack([labels[:TOK_DEV], labels[TOK_DEV:]], axis=1)
        slots_sorted = jnp.stack([slot_values[:TOK_DEV], slot_values[TOK_DEV:]], axis=1)
        ids_block = jnp.zeros((TOK_DEV, 2), jnp.int32).at[order].set(ids_sorted)
        slots_block = jnp.zeros((TOK_DEV, 2), jnp.int32).at[order].set(slots_sorted)
        return (ids_block, slots_block)
    ids_all, slots_all = lax.map(one_block, jnp.arange(blocks, dtype=jnp.int32))
    return (ids_all.reshape(TOKENS, 2), slots_all.reshape(TOKENS, 2))


def draw_expert_ids(key, part):
    return route_table(jax.random.fold_in(key, 7))[0]


def draw_expert_slots(key, part):
    return route_table(jax.random.fold_in(key, 7))[1]


def draw_expert_capacity(key, part):
    base_key = jax.random.fold_in(key, 7)
    limits = jax.random.randint(jax.random.fold_in(key, 29), (EXPERTS,), CAP // 2, CAP + 1).astype(jnp.int32)
    chosen = hot_expert(base_key, 0)
    return jnp.where(jnp.arange(EXPERTS, dtype=jnp.int32) == chosen, CAP, limits).astype(jnp.int32)


def draw_keep_mask(key, part):
    position = jnp.arange(TOKENS, dtype=jnp.int32)
    threshold = 250 + 750 * position // TOKENS
    coins = jax.random.randint(jax.random.fold_in(key, 23), (TOKENS, 2), 0, 1000)
    return (coins < threshold[:, None]).astype(jnp.int32)


def draw_block_input(key, part):
    keys_list = jax.random.split(jax.random.fold_in(key, 37), 4)
    position = jnp.arange(TOKENS, dtype=jnp.float32) / TOKENS
    common = jax.random.truncated_normal(keys_list[0], -4.0, 4.0, (D,), jnp.float32)
    noise = jax.random.truncated_normal(keys_list[1], -4.0, 4.0, (TOKENS, D), jnp.float32)
    row_scales = jnp.exp(jax.random.uniform(keys_list[2], (TOKENS,), jnp.float32, math.log(0.3), math.log(3.0)))
    leaning = 1.2 * position
    column_scales = jnp.exp(jax.random.uniform(keys_list[3], (D,), jnp.float32, math.log(0.4), math.log(2.5)))
    values = row_scales[:, None] * (noise * column_scales[None, :] + leaning[:, None] * common[None, :])
    return values.astype(jnp.bfloat16)


def shard_levels(own_key, extent, cuts, low, top_value):
    level, own = 1.0, jax.random.fold_in(own_key, 6)
    for axis_at, shards_of in cuts:
        heights = jnp.exp(jax.random.uniform(jax.random.fold_in(own, axis_at), (shards_of,), jnp.float32, low / len(cuts), top_value / len(cuts)))
        level = level * jnp.repeat(heights, extent[axis_at] // shards_of).reshape([-1 if axis == axis_at else 1 for axis in range(len(extent))])
    return level


def bell_draw(own_key, shape, width, most, pieces=(), kind=jnp.bfloat16):
    entries = jax.random.normal(own_key, shape, jnp.float32) * width
    if len(pieces) > 0:
        entries = shard_levels(own_key, shape, pieces, -0.22, 0.18) * entries
    return jnp.clip(entries, min=-most, max=most).astype(kind)


def setup_inputs(seed: int = 0) -> dict:
    key_list = jax.random.split(jax.random.key(seed), 14)
    return {
        "block_input": draw_block_input(jax.random.fold_in(key_list[13], 71), 0),
        "attention_in": bell_draw(key_list[1], (D, 3 * D), D ** -0.5, 0.21875, ((0, 16), (1, 2))),
        "attention_out": bell_draw(key_list[2], (D, D), (D // 16) ** -0.5, 0.875, ((0, 16), (1, 2))),
        "expert_up": bell_draw(key_list[3], (EXPERTS, D, FF), D ** -0.5, 0.21875, ((0, 16), (1, 2))),
        "expert_down": bell_draw(key_list[4], (EXPERTS, FF, D), 2 ** -0.5, 4.0, ((0, 16), (2, 2))),
        "router_weight": bell_draw(key_list[5], (D, EXPERTS), (4 * D) ** -0.5, 0.109375, (), jnp.float32),
        "gain_attention": jnp.clip(1.0 + 0.15 * jax.random.normal(key_list[6], (D,), jnp.float32), 0.25, 1.75),
        "gain_experts": jnp.clip(1.0 + 0.15 * jax.random.normal(key_list[7], (D,), jnp.float32), 0.25, 1.75),
        "expert_ids": draw_expert_ids(jax.random.fold_in(key_list[13], 71), 0),
        "expert_slots": draw_expert_slots(jax.random.fold_in(key_list[13], 71), 0),
        "expert_capacity": draw_expert_capacity(jax.random.fold_in(key_list[13], 71), 0),
        "keep_mask": draw_keep_mask(jax.random.fold_in(key_list[13], 71), 0),
        "output_grad": bell_draw(key_list[12], (TOKENS, D), 1.0, 6.0, ((0, 32),)),
    }


@jax.custom_vjp
def low(v):
    return lax.optimization_barrier(v.astype(jnp.bfloat16)).astype(jnp.float32)

@jax.custom_vjp
def low_back(v):
    return v

def low_keep(v):
    return (low(v), None)

def low_pass(kept, grad):
    return (grad,)

def back_keep(v):
    return (v, None)

def back_low(kept, grad):
    return (low(grad),)
low.defvjp(low_keep, low_pass)
low_back.defvjp(back_keep, back_low)
epsilon = 1e-06
highest = lax.Precision.HIGHEST

def norm_rows(values, gain_vector):
    centred = values - lax.optimization_barrier(jnp.mean(values, axis=-1, keepdims=True))
    inv_scale = lax.rsqrt(lax.optimization_barrier(jnp.mean(centred * centred, axis=-1, keepdims=True)) + epsilon)
    return centred * inv_scale * gain_vector

def gelu_exact(values):
    return 0.5 * values * (1.0 + lax.erf(values * 0.7071067811865476))

def route_gates(normed, router_weight, expert_ids):
    logits = jnp.dot(normed, router_weight, precision=highest)
    shifted = jnp.exp(logits - lax.optimization_barrier(jnp.max(logits, axis=-1, keepdims=True)))
    router_probs = shifted / lax.optimization_barrier(jnp.sum(shifted, axis=-1, keepdims=True))
    return jnp.take_along_axis(router_probs, expert_ids, axis=1)

def attend_group(group_parts):
    queries, keys_part, values_part = group_parts
    scores = low_back(jnp.einsum('iqhd,ikhd->ihqk', queries, keys_part, precision=highest) * 0.125)
    row_max = lax.optimization_barrier(jnp.max(scores, axis=-1, keepdims=True))
    powered = jnp.exp(scores - row_max)
    attn_probs = powered / lax.optimization_barrier(jnp.sum(powered, axis=-1, keepdims=True))
    return jnp.einsum('ihqk,ikhd->iqhd', low(attn_probs), values_part, precision=highest)

def expert_apply(expert_parts):
    expert_rows, up_matrix, down_matrix = expert_parts
    inner_act = low_back(jnp.dot(expert_rows, up_matrix, precision=highest))
    hidden = low(gelu_exact(inner_act))
    return low(low_back(jnp.dot(hidden, down_matrix, precision=highest)))

def reference(block_input, attention_in, attention_out, expert_up, expert_down, router_weight, gain_attention, gain_experts, expert_ids, expert_slots, expert_capacity, keep_mask, output_grad):
    blocks = TOKENS // TOK_DEV
    token_index = jnp.arange(TOKENS, dtype=jnp.int32)
    limit_pairs = expert_capacity[expert_ids]
    used_pairs = (keep_mask == 1) & (expert_slots < limit_pairs)
    buffer_rows = EXPERTS * blocks * CAP
    block_index = token_index // TOK_DEV
    slot_index = jnp.where(used_pairs, (expert_ids * blocks + block_index[:, None]) * CAP + expert_slots, buffer_rows).astype(jnp.int32)
    token_table = jnp.full((buffer_rows + 1,), TOKENS, jnp.int32).at[slot_index.reshape(-1)].set(jnp.repeat(token_index, 2))[:buffer_rows]
    group_size = 4 * IMG_DEV

    def forward(source, in_matrix, out_matrix, up_matrices, down_matrices, router_matrix, gain_one, gain_two):
        normed_one = low(norm_rows(source, gain_one))
        projected = low(low_back(jnp.dot(normed_one, in_matrix, precision=highest)))
        shaped = projected.reshape(IMAGES // group_size, group_size, SEQ, 3, HEADS, HEAD_DIM)
        mixed_groups = lax.map(jax.checkpoint(attend_group), (shaped[:, :, :, 0], shaped[:, :, :, 1], shaped[:, :, :, 2]))
        mixed = low(low_back(mixed_groups.reshape(TOKENS, D)))
        branch_attn = low_back(jnp.dot(mixed, out_matrix, precision=highest))
        residual = source + branch_attn
        normed_two = norm_rows(residual, gain_two)
        sent_rows = low(normed_two)
        gate_values = route_gates(normed_two, router_matrix, expert_ids)
        padded = jnp.concatenate([sent_rows, jnp.zeros((1, D), jnp.float32)], axis=0)
        expert_rows = low_back(padded[token_table]).reshape(EXPERTS, blocks * CAP, D)
        returned = lax.map(jax.checkpoint(expert_apply), (expert_rows, up_matrices, down_matrices))
        padded_back = jnp.concatenate([returned.reshape(buffer_rows, D), jnp.zeros((1, D), jnp.float32)], axis=0)
        picked = padded_back[slot_index]
        weights_used = jnp.where(used_pairs, gate_values, 0.0)
        branch_moe = lax.optimization_barrier(jnp.sum(weights_used[:, :, None] * picked, axis=1))
        result = residual + branch_moe
        statistics = jnp.sqrt(jnp.stack([jnp.mean(result * result), jnp.mean(branch_attn * branch_attn), jnp.mean(branch_moe * branch_moe)]))
        return (result, statistics)
    floats = (block_input.astype(jnp.float32), attention_in.astype(jnp.float32), attention_out.astype(jnp.float32), expert_up.astype(jnp.float32), expert_down.astype(jnp.float32), router_weight, gain_attention, gain_experts)
    result, pullback, statistics = jax.vjp(forward, *floats, has_aux=True)
    gradients = pullback(output_grad.astype(jnp.float32))
    return (result.astype(jnp.bfloat16), gradients[0].astype(jnp.bfloat16), gradients[1], gradients[2], gradients[3], gradients[4], gradients[5], gradients[6], gradients[7], statistics)
```

```python
import functools

import jax
import jax.numpy as jnp
from jax import lax
from jax.experimental import pallas as pl
from jax.experimental.pallas import tpu as pltpu
from jax.sharding import PartitionSpec as P

HEADS = 12
HEAD_DIM = 64
SEQ = 197
EPS = 1e-06
F32 = jnp.float32
BF16 = jnp.bfloat16
WIN = 224
STEP = 192
NEG = -1e30
MIB = 1 << 20

VMEM = pl.BlockSpec(memory_space=pltpu.VMEM)
ANY = pl.BlockSpec(memory_space=pl.ANY)
MESH = pl.DeviceIdType.MESH
DMA = pltpu.SemaphoreType.DMA


def dot(a, b):
    return jnp.dot(a, b, preferred_element_type=F32)


def dot_nt(a, b):
    return lax.dot_general(a, b, (((1,), (1,)), ((), ())), preferred_element_type=F32)


def dot_tn(a, b):
    return lax.dot_general(a, b, (((0,), (0,)), ((), ())), preferred_element_type=F32)


def cdiv(a, b):
    return (a + b - 1) // b


def params(mib, **kw):
    return pltpu.CompilerParams(vmem_limit_bytes=mib * MIB, **kw)


def split_bf16(v):
    hi = v.astype(BF16)
    return hi, (v - hi.astype(F32)).astype(BF16)


def load_blocks(g_hbm, dst, sem):
    blocks, rh, cw = g_hbm.shape
    nc = dst.shape[1] // cw
    for b in range(blocks):
        r, c = divmod(b, nc)
        pltpu.make_async_copy(
            g_hbm.at[b], dst.at[pl.ds(r * rh, rh), pl.ds(c * cw, cw)], sem
        ).start()


def wait_all(dst, sem):
    pltpu.make_async_copy(dst, dst, sem).wait()


def row_loop(total, step, body):
    @pl.loop(0, total // step)
    def _(i):
        body(pl.ds(pl.multiple_of(i * step, step), step))


def pad_rows(src_ref, dst_ref):
    rows, padded = src_ref.shape[0], dst_ref.shape[0]
    tail = rows // 16 * 16
    dst_ref[tail:padded, :] = jnp.zeros((padded - tail, dst_ref.shape[1]), dst_ref.dtype)
    dst_ref[0:rows, :] = src_ref[...]


def norm_parts(v):
    c = v - jnp.mean(v, axis=-1, keepdims=True)
    r = lax.rsqrt(jnp.mean(c * c, axis=-1, keepdims=True) + EPS)
    return c * r, r


def slot_hits(slot_ref, base, rows):
    lanes = slot_ref.shape[1]
    at = lax.broadcasted_iota(jnp.int32, (rows, lanes), 0) + base
    return at == slot_ref[0:1, :], at == slot_ref[1:2, :]


def mesh_place():
    r, c = lax.axis_index("row"), lax.axis_index("col")
    return r // 4, (r // 2) % 2, r % 2, c


def device(z, y, k, c):
    return {"row": z * 4 + y * 2 + k, "col": c}


def greet(peers):
    barrier = pltpu.get_barrier_semaphore()
    for peer in peers:
        pl.semaphore_signal(barrier, inc=1, device_id=peer, device_id_type=MESH)
    pl.semaphore_wait(barrier, len(peers))


def push(src, dst, send, recv, peer):
    copy = pltpu.make_async_remote_copy(
        src_ref=src, dst_ref=dst, send_sem=send, recv_sem=recv, device_id=peer, device_id_type=MESH
    )
    copy.start()
    return copy


def zflip(z, d):
    bit0, bit1 = z % 2, z // 2
    if d & 1:
        bit0 = 1 - bit0
    if d & 2:
        bit1 = 1 - bit1
    return bit1 * 2 + bit0


def peers_of(z, y, k, c):
    return [device(zflip(z, d), y, k, c) for d in (1, 2, 3)] + [
        device(z, y, 1 - k, c), device(z, y, k, 1 - c), device(z, 1 - y, k, c)
    ]


def gather_kernel(own_ref, g_ref, zs, zr, xs, xr, ys, yr, ks, kr, own_sem):
    z, y, k, c = mesh_place()
    rh, half = own_ref.shape[0], own_ref.shape[1] // 2
    greet(peers_of(z, y, k, c))
    across, up, twin = device(z, y, k, 1 - c), device(z, 1 - y, k, c), device(z, y, 1 - k, c)

    def at(zz, yy, kk, cc, cols=None):
        rows = pl.ds(pl.multiple_of((zz * 4 + yy * 2 + kk) * rh, rh), rh)
        if cols is None:
            return g_ref.at[cc, rows, :]
        return g_ref.at[cc, rows, cols]

    h1, h2 = pl.ds(0, half), pl.ds(half, half)
    mine = at(z, y, k, c)
    zc = [push(own_ref, mine, zs.at[d - 1], zr.at[d - 1], device(zflip(z, d), y, k, c)) for d in (1, 2, 3)]
    keep = pltpu.make_async_copy(own_ref, mine, own_sem)
    keep.start()
    sent = list(zc)
    xc, yc, kc, xf, yf = [], [], [], [], []
    for d in range(4):
        zz = zflip(z, d)
        if d:
            zc[d - 1].wait_recv()
        src = own_ref if d == 0 else at(zz, y, k, c)
        xc.append(push(src, at(zz, y, k, c), xs.at[d], xr.at[d], across))
        yc.append(push(src, at(zz, y, k, c), ys.at[d], yr.at[d], up))
        kc.append(push(src, at(zz, y, k, c), ks.at[d], kr.at[d], twin))
    for d in range(4):
        zz = zflip(z, d)
        xc[d].wait_recv()
        src = at(zz, y, k, 1 - c)
        yf.append(push(at(zz, y, k, 1 - c, h1), at(zz, y, k, 1 - c, h1), ys.at[4 + d], yr.at[4 + d], up))
        kc.append(push(src, src, ks.at[4 + d], kr.at[4 + d], twin))
        yc[d].wait_recv()
        src = at(zz, 1 - y, k, c)
        xf.append(push(at(zz, 1 - y, k, c, h2), at(zz, 1 - y, k, c, h2), xs.at[4 + d], xr.at[4 + d], across))
        kc.append(push(src, src, ks.at[8 + d], kr.at[8 + d], twin))
    for d in range(4):
        yf[d].wait_recv()
        xf[d].wait_recv()
        src = at(zflip(z, d), 1 - y, k, 1 - c)
        kc.append(push(src, src, ks.at[12 + d], kr.at[12 + d], twin))
    for copy in kc:
        copy.wait_recv()
    for copy in zc + xc + yc + xf + yf + kc:
        copy.wait_send()
    keep.wait()


def reduce_kernel(
    w_ref, small_ref, out_ref, small_out,
    rk, acc, rx2, ry2, rx3, ry3, rz, cur, rs,
    ks, kr, xs, xr, ys, yr, zs, zr, ss, sr,
):
    z, y, k, c = mesh_place()
    rh, half = out_ref.shape[0], out_ref.shape[1] // 2
    greet(peers_of(z, y, k, c))
    across, up, twin = device(z, y, k, 1 - c), device(z, 1 - y, k, c), device(z, y, 1 - k, c)
    order = (3, 2, 1, 0)
    lo, hi = pl.ds(0, half), pl.ds(half, half)

    def rows(zz, yy, kk):
        return pl.ds(pl.multiple_of((zz * 4 + yy * 2 + kk) * rh, rh), rh)

    chain = [twin, across, up, device(zflip(z, 1), y, k, c), device(zflip(z, 2), y, k, c)]
    small = []
    cur[0] = small_ref[...]

    def small_send():
        j = len(small)
        small.append(push(cur.at[j], rs.at[j], ss.at[j], sr.at[j], chain[j]))

    def small_take():
        j = len(small) - 1
        small[j].wait_recv()
        cur[j + 1] = cur[j] + rs[j]

    kc = {}
    for d in order:
        zz = zflip(z, d)
        for yy in range(2):
            for cc in range(2):
                n = yy * 2 + cc
                kc[d, yy, cc] = push(
                    w_ref.at[cc, rows(zz, yy, 1 - k), :], rk.at[d, yy, cc], ks.at[d * 4 + n], kr.at[d * 4 + n], twin
                )
    small_send()
    c2x, c2y, c3x, c3y, cz = {}, {}, {}, {}, {}
    for d in order:
        zz = zflip(z, d)
        for yy in range(2):
            for cc in range(2):
                kc[d, yy, cc].wait_recv()
                acc[d, yy, cc] = (
                    w_ref[cc, rows(zz, yy, k), :].astype(F32) + rk[d, yy, cc].astype(F32)
                ).astype(BF16)
        c2y[d] = push(acc.at[d, 1 - y, :, :, lo], ry2.at[d], ys.at[d], yr.at[d], up)
        c2x[d] = push(acc.at[d, :, 1 - c, :, hi], rx2.at[d], xs.at[d], xr.at[d], across)
    small_take()
    small_send()
    for d in order:
        c2y[d].wait_recv()
        for cc in range(2):
            acc[d, y, cc, :, 0:half] = (
                acc[d, y, cc, :, 0:half].astype(F32) + ry2[d, cc].astype(F32)
            ).astype(BF16)
        c3x[d] = push(acc.at[d, y, 1 - c, :, lo], rx3.at[d], xs.at[4 + d], xr.at[4 + d], across)
        c2x[d].wait_recv()
        for yy in range(2):
            acc[d, yy, c, :, half:] = (
                acc[d, yy, c, :, half:].astype(F32) + rx2[d, yy].astype(F32)
            ).astype(BF16)
        c3y[d] = push(acc.at[d, 1 - y, c, :, hi], ry3.at[d], ys.at[4 + d], yr.at[4 + d], up)
    small_take()
    small_send()
    for d in order:
        c3x[d].wait_recv()
        acc[d, y, c, :, 0:half] = (
            acc[d, y, c, :, 0:half].astype(F32) + rx3[d].astype(F32)
        ).astype(BF16)
        c3y[d].wait_recv()
        acc[d, y, c, :, half:] = (
            acc[d, y, c, :, half:].astype(F32) + ry3[d].astype(F32)
        ).astype(BF16)
        if d:
            cz[d] = push(acc.at[d, y, c], rz.at[d - 1], zs.at[d - 1], zr.at[d - 1], device(zflip(z, d), y, k, c))
    small_take()
    small_send()
    small_take()
    small_send()
    total = acc[0, y, c].astype(F32)
    for d in (1, 2, 3):
        cz[d].wait_recv()
        total += rz[d - 1].astype(F32)
    out_ref[...] = total
    small[4].wait_recv()
    small_out[...] = cur[4] + rs[4]
    for group in (kc, c2x, c2y, c3x, c3y, cz):
        for copy in group.values():
            copy.wait_send()
    for copy in small:
        copy.wait_send()


def dispatch_kernel(blocks, src_ref, slot_ref, out_ref, pad):
    pad_rows(src_ref, pad)
    rows = out_ref.shape[0] // blocks

    @pl.loop(0, blocks)
    def _(b):
        base = pl.multiple_of(b * rows, 16)
        h0, h1 = slot_hits(slot_ref, base, rows)
        pick = jnp.where(h0 | h1, 1.0, 0.0).astype(BF16)
        out_ref[pl.ds(base, rows), :] = dot(pick, pad[...]).astype(BF16)


def forward_kernel(
    images, experts, blocks,
    x_ref, wt_ref, g1_ref, g2_ref, rw_ref, slot_ref,
    proj_ref, mixed_ref, lse_ref, res_ref, probs_ref, tok_ref, sq_ref,
    n1, xs, sent, low,
):
    padded, width = xs.shape
    nc = wt_ref.shape[0]
    cw, ow = 3 * width // nc, width // nc
    pad_rows(x_ref, xs)

    def norm_one(rows):
        n, _ = norm_parts(xs[rows, :].astype(F32))
        n1[rows, :] = (n * g1_ref[...]).astype(BF16)

    row_loop(padded, 32, norm_one)
    mixed_ref[...] = jnp.zeros_like(mixed_ref)
    lse_ref[...] = jnp.zeros_like(lse_ref)
    for c in range(nc):
        proj_ref[:, c * cw : (c + 1) * cw] = dot(n1[...], wt_ref[c, :, 0:cw]).astype(BF16)

    lane = lax.broadcasted_iota(jnp.int32, (1, 128), 1)
    first = lane < HEAD_DIM
    key_at = lax.broadcasted_iota(jnp.int32, (1, WIN), 1)
    row_at = lax.broadcasted_iota(jnp.int32, (WIN, 1), 0)

    @pl.loop(0, HEADS // 2)
    def _(p):
        qc = pl.ds(pl.multiple_of(p * 128, 128), 128)
        kc = pl.ds(pl.multiple_of(width + p * 128, 128), 128)
        vc = pl.ds(pl.multiple_of(2 * width + p * 128, 128), 128)
        for i in range(images):
            rows = slice(STEP * i, STEP * i + WIN)
            off = (SEQ - STEP) * i
            bias = jnp.where((key_at >= off) & (key_at < off + SEQ), 0.0, NEG)
            valid = (row_at >= off) & (row_at < off + SEQ)
            q = (proj_ref[rows, qc].astype(F32) * 0.125)
            qq = jnp.concatenate([jnp.where(first, q, 0.0), jnp.where(first, 0.0, q)], axis=0).astype(BF16)
            s = dot_nt(qq, proj_ref[rows, kc]) + bias
            top = jnp.max(s, axis=1, keepdims=True)
            e = jnp.exp(s - top)
            total = jnp.sum(e, axis=1, keepdims=True)
            o = dot(e.astype(BF16), proj_ref[rows, vc]) / total
            lse = top + jnp.log(total)
            om = jnp.where(first, o[:WIN], o[WIN:])
            old = mixed_ref[rows, qc].astype(F32)
            mixed_ref[rows, qc] = jnp.where(valid, om, old).astype(BF16)
            ls = lse_ref[rows, :]
            ls = jnp.where(valid & (lane == 2 * p), lse[:WIN], ls)
            lse_ref[rows, :] = jnp.where(valid & (lane == 2 * p + 1), lse[WIN:], ls)

    for c in range(nc):
        cols = slice(c * ow, (c + 1) * ow)
        branch = dot(mixed_ref[...], wt_ref[c, :, cw:])
        sq_ref[:, cols] = jnp.sum(branch * branch, axis=0, keepdims=True)
        res_ref[:, cols] = xs[:, cols].astype(F32) + branch

    def norm_two(rows):
        n, _ = norm_parts(res_ref[rows, :])
        v = n * g2_ref[...]
        hi, lo = split_bf16(v)
        sent[rows, :] = hi
        low[rows, :] = lo

    row_loop(padded, 32, norm_two)
    rw_hi, rw_lo = split_bf16(rw_ref[...])
    both = dot_nt(jnp.concatenate([rw_hi, rw_lo], axis=0), sent[...])
    logits = both[:experts] + both[experts:] + dot_nt(rw_hi, low[...])
    e = jnp.exp(logits - jnp.max(logits, axis=0, keepdims=True))
    probs = e / jnp.sum(e, axis=0, keepdims=True)
    probs_ref[...] = probs
    rows = tok_ref.shape[0] // blocks

    @pl.loop(0, blocks)
    def _(b):
        base = pl.multiple_of(b * rows, 16)
        h0, h1 = slot_hits(slot_ref, base, rows)
        pick = jnp.where(h0 | h1, 1.0, 0.0).astype(BF16)
        tok_ref[pl.ds(base, rows), :] = dot(pick, sent[...]).astype(BF16)


def gelu_both(v):
    phi = 0.5 * (1.0 + lax.erf(v * 0.7071067811865476))
    slope = phi + v * jnp.exp(-0.5 * v * v) * 0.3989422804014327
    return v * phi, slope


def expert_kernel(
    fstep, srcs, cap,
    x_ref, og_ref, rw_ref, up_hbm, down_hbm,
    ret_ref, gs_ref, h_ref, gi_ref, gr_ref, gg_ref,
    up, down, acc, gacc, ggc, sem_up, sem_down,
):
    b = pl.program_id(0)

    @pl.when(b == 0)
    def _():
        load_blocks(up_hbm, up, sem_up)
        load_blocks(down_hbm, down, sem_down)
        ggc[...] = jnp.zeros_like(ggc)
        wait_all(up, sem_up)
        wait_all(down, sem_down)

    lane = lax.broadcasted_iota(jnp.int32, (1, 128), 1)
    experts = rw_ref.shape[1]
    x = x_ref[...]
    rw_hi, rw_lo = split_bf16(rw_ref[...])
    logits = dot(x, rw_hi) + dot(x, rw_lo)
    e = jnp.exp(logits - jnp.max(logits, axis=1, keepdims=True))
    own = lax.broadcasted_iota(jnp.int32, (1, experts), 1) == lax.axis_index("row")
    w = jnp.sum(jnp.where(own, e, 0.0), axis=1, keepdims=True) / jnp.sum(e, axis=1, keepdims=True)
    gr_ref[...] = (og_ref[...].astype(F32) * w).astype(BF16)
    acc[...] = jnp.zeros_like(acc)
    gacc[...] = jnp.zeros_like(gacc)

    @pl.loop(0, up.shape[1] // fstep)
    def _(f):
        cols = pl.ds(pl.multiple_of(f * fstep, fstep), fstep)
        inner = dot(x_ref[...], up[:, cols])
        hid, slope = gelu_both(inner)
        hid = hid.astype(BF16)
        h_ref[:, cols] = hid
        gh = dot_nt(gr_ref[...], down[cols, :])
        gi = (gh * slope).astype(BF16)
        gi_ref[:, cols] = gi
        acc[...] += dot(hid, down[cols, :])
        gacc[...] += dot_nt(gi, up[:, cols])

    gs_ref[...] = gacc[...].astype(BF16)
    ret = acc[...]
    ret_ref[...] = (w * ret).astype(BF16)
    gg = jnp.sum(ret.astype(BF16).astype(F32) * og_ref[...].astype(F32), axis=1, keepdims=True)
    old = ggc[0:cap, :]
    for s in range(srcs):
        old = jnp.where(lane == b * srcs + s, gg[s * cap : (s + 1) * cap], old)
    ggc[0:cap, :] = old

    @pl.when(b == pl.num_programs(0) - 1)
    def _():
        gg_ref[...] = jnp.transpose(ggc[...])[0 : gg_ref.shape[0], :]


def weight_grad_kernel(x_ref, gr_ref, h_ref, gi_ref, up_ref, down_ref, xt):
    @pl.when(pl.program_id(0) == 0)
    def _():
        xt[...] = jnp.transpose(x_ref[...])

    up = dot(xt[...], gi_ref[...]).astype(BF16)
    half = up_ref.shape[1]
    for c in range(up_ref.shape[0]):
        up_ref[c, :, :] = up[c * half : (c + 1) * half, :]
    down = dot_tn(h_ref[...], gr_ref[...]).astype(BF16)
    wide = down_ref.shape[2]
    for c in range(down_ref.shape[0]):
        down_ref[c, :, :] = down[:, c * wide : (c + 1) * wide]


def build_combine(slotc_ref, comb):
    padded, slots = comb.shape
    s0 = jnp.broadcast_to(slotc_ref[:, 0:1], (padded, 128))
    s1 = jnp.broadcast_to(slotc_ref[:, 1:2], (padded, 128))
    at = lax.broadcasted_iota(jnp.int32, (padded, 128), 1)

    @pl.loop(0, slots // 128)
    def _(j):
        here = at + j * 128
        cols = pl.ds(pl.multiple_of(j * 128, 128), 128)
        comb[:, cols] = jnp.where((s0 == here) | (s1 == here), 1.0, 0.0).astype(BF16)


def backward_kernel(
    images, experts,
    x_ref, og_ref, wt_ref, g1_ref, g2_ref, rw_ref, slot_ref, slotc_ref,
    proj_ref, mixed_ref, lse_ref, res_ref, probs_ref, gback_ref, gg_ref,
    xgrad_ref, wgrad_ref, rgrad_ref, gains_ref,
    xs, ogs, comb, big, gres, gb, gmix, gproj, n1, glt, gcol, gacc,
):
    padded, width = xs.shape
    pad_rows(x_ref, xs)
    pad_rows(og_ref, ogs)
    cap = gback_ref.shape[0] // experts
    build_combine(slotc_ref, comb)

    gcol[...] = jnp.zeros_like(gcol)
    gcol[0:experts, :] = gg_ref[...]
    gt = jnp.transpose(gcol[...])[0:cap]
    expert_at = lax.broadcasted_iota(jnp.int32, (experts, padded), 0)
    held = jnp.zeros((experts, padded), F32)
    for e in range(experts):
        h0, h1 = slot_hits(slot_ref, e * cap, cap)
        row = jnp.sum(jnp.where(h0 | h1, gt[:, e : e + 1], 0.0), axis=0, keepdims=True)
        held = jnp.where(expert_at == e, row, held)
    probs = probs_ref[...]
    gl = probs * (held - jnp.sum(probs * held, axis=0, keepdims=True))
    gl_hi, gl_lo = split_bf16(gl)
    rw_hi, rw_lo = split_bf16(rw_ref[...])
    glt[...] = jnp.concatenate([gl_hi, gl_lo, gl_hi], axis=0)
    rw3 = jnp.concatenate([rw_hi, rw_hi, rw_lo], axis=0)

    @pl.loop(0, width // 256)
    def _(j):
        cols = pl.ds(pl.multiple_of(j * 256, 256), 256)
        big[:, cols] = dot(comb[...], gback_ref[:, cols])

    for j in range(width // 256):
        cols = slice(j * 256, (j + 1) * 256)
        big[:, cols] = big[:, cols] + dot_tn(glt[...], rw3[:, cols])

    gacc[...] = jnp.zeros_like(gacc)

    def norm_two(rows):
        n, r = norm_parts(res_ref[rows, :])
        g = big[rows, :]
        u = g * g2_ref[...]
        back = r * (
            u - jnp.mean(u, axis=-1, keepdims=True) - n * jnp.mean(u * n, axis=-1, keepdims=True)
        )
        total = ogs[rows, :].astype(F32) + back
        gres[rows, :] = total
        gb[rows, :] = total.astype(BF16)
        n1[rows, :] = (n * g2_ref[...]).astype(BF16)
        gacc[0:8, :] += jnp.sum((g * n).reshape(-1, 8, width), axis=0)

    row_loop(padded, 32, norm_two)
    both = dot(jnp.concatenate([gl_hi, gl_lo], axis=0), n1[...])
    rgrad_ref[...] = both[:experts] + both[experts:]
    nc = wt_ref.shape[0]
    cw, ow = 3 * width // nc, width // nc
    for c in range(nc):
        wgrad_ref[c, :, cw:] = dot_tn(mixed_ref[...], gb[:, c * ow : (c + 1) * ow]).astype(BF16)
    gmix[...] = sum(
        dot_nt(gb[:, c * ow : (c + 1) * ow], wt_ref[c, :, cw:]) for c in range(nc)
    ).astype(BF16)

    def norm_one(rows):
        n, _ = norm_parts(xs[rows, :].astype(F32))
        n1[rows, :] = (n * g1_ref[...]).astype(BF16)

    row_loop(padded, 32, norm_one)
    gproj[...] = jnp.zeros_like(gproj)
    lane = lax.broadcasted_iota(jnp.int32, (1, 128), 1)
    first = lane < HEAD_DIM
    key_at = lax.broadcasted_iota(jnp.int32, (1, WIN), 1)
    row_at = lax.broadcasted_iota(jnp.int32, (WIN, 1), 0)

    def stack(v):
        return jnp.concatenate([jnp.where(first, v, 0.0), jnp.where(first, 0.0, v)], axis=0).astype(BF16)

    @pl.loop(0, HEADS // 2)
    def _(p):
        qc = pl.ds(pl.multiple_of(p * 128, 128), 128)
        kc = pl.ds(pl.multiple_of(width + p * 128, 128), 128)
        vc = pl.ds(pl.multiple_of(2 * width + p * 128, 128), 128)
        for i in range(images):
            rows = slice(STEP * i, STEP * i + WIN)
            off = (SEQ - STEP) * i
            bias = jnp.where((key_at >= off) & (key_at < off + SEQ), 0.0, NEG)
            valid = (row_at >= off) & (row_at < off + SEQ)
            qq = stack(proj_ref[rows, qc].astype(F32) * 0.125)
            k = proj_ref[rows, kc]
            v = proj_ref[rows, vc]
            gg = stack(gmix[rows, qc].astype(F32))
            ls = lse_ref[rows, :]
            l0 = jnp.sum(jnp.where(lane == 2 * p, ls, 0.0), axis=1, keepdims=True)
            l1 = jnp.sum(jnp.where(lane == 2 * p + 1, ls, 0.0), axis=1, keepdims=True)
            lse = jnp.concatenate([jnp.where(valid, l0, -NEG), jnp.where(valid, l1, -NEG)], axis=0)
            pr = jnp.exp(dot_nt(qq, k) + bias - lse)
            gp = dot_nt(gg, v)
            delta = jnp.sum(pr * gp, axis=1, keepdims=True)
            gs = (pr * (gp - delta)).astype(BF16)
            gq2 = dot(gs, k)
            gq = jnp.where(first, gq2[:WIN], gq2[WIN:]) * 0.125
            gk = dot_tn(gs, qq)
            gv = dot_tn(pr.astype(BF16), gg)
            for cols, val in ((qc, gq), (kc, gk), (vc, gv)):
                old = gproj[rows, cols].astype(F32)
                gproj[rows, cols] = jnp.where(valid, val, old).astype(BF16)

    for c in range(nc):
        cols = slice(c * cw, (c + 1) * cw)
        wgrad_ref[c, :, 0:cw] = dot_tn(n1[...], gproj[:, cols]).astype(BF16)
    big[...] = sum(
        dot_nt(gproj[:, c * cw : (c + 1) * cw], wt_ref[c, :, 0:cw]) for c in range(nc)
    )
    gacc[8:16, :] = jnp.zeros((8, width), F32)

    def norm_one_back(rows):
        n, r = norm_parts(xs[rows, :].astype(F32))
        g = big[rows, :]
        u = g * g1_ref[...]
        back = r * (
            u - jnp.mean(u, axis=-1, keepdims=True) - n * jnp.mean(u * n, axis=-1, keepdims=True)
        )
        gb[rows, :] = (gres[rows, :] + back).astype(BF16)
        gacc[8:16, :] += jnp.sum((g * n).reshape(-1, 8, width), axis=0)

    row_loop(padded, 32, norm_one_back)
    xgrad_ref[...] = gb[0 : xgrad_ref.shape[0], :]
    gains_ref[...] = jnp.concatenate(
        [
            jnp.sum(gacc[8:16, :], axis=0, keepdims=True),
            jnp.sum(gacc[0:8, :], axis=0, keepdims=True),
        ],
        axis=0,
    )


def combine_kernel(slotc_ref, res_ref, back_ref, out_ref, sq_ref, comb, acc):
    build_combine(slotc_ref, comb)

    @pl.loop(0, acc.shape[1] // 256)
    def _(j):
        cols = pl.ds(pl.multiple_of(j * 256, 256), 256)
        branch = dot(comb[...], back_ref[:, cols])
        result = res_ref[:, cols] + branch
        acc[:, cols] = result.astype(BF16)
        sq_ref[0:1, cols] = jnp.sum(result * result, axis=0, keepdims=True)
        sq_ref[1:2, cols] = jnp.sum(branch * branch, axis=0, keepdims=True)

    out_ref[...] = acc[0 : out_ref.shape[0], :]


def shape(dims, dtype=BF16):
    return jax.ShapeDtypeStruct(dims, dtype)


def per_device(
    block_input, attention_in, attention_out, expert_up, expert_down, router_weight,
    gain_attention, gain_experts, expert_ids, expert_slots, expert_capacity, keep_mask, output_grad,
):
    tokens, width = block_input.shape
    images = tokens // SEQ
    padded = STEP * images + (WIN - STEP)
    experts = expert_capacity.shape[0]
    cap = (2 * tokens * 11 // (8 * experts) + 7) // 8 * 8
    slots = experts * cap
    cap_lanes = cdiv(cap, 128) * 128
    nrow, ncol = lax.axis_size("row"), lax.axis_size("col")
    ff = expert_up.shape[2]
    blocks = 4
    aligned = (width // ncol) % 128 == 0

    ring = nrow == 16 and ncol == 2
    own_weights = jnp.concatenate([attention_in, attention_out], axis=1)
    rh, wcols = own_weights.shape
    if ring:
        weights = pl.pallas_call(
            gather_kernel,
            out_shape=shape((ncol, width, wcols)),
            in_specs=[VMEM],
            out_specs=VMEM,
            scratch_shapes=[DMA((3,)), DMA((3,)), DMA((8,)), DMA((8,)), DMA((8,)), DMA((8,)),
                            DMA((16,)), DMA((16,)), DMA],
            compiler_params=params(24, collective_id=0, has_side_effects=True),
            name="attn_weights_gather",
        )(own_weights)
    else:
        weights = jnp.concatenate(
            [
                lax.all_gather(lax.all_gather(v, "col", axis=1, tiled=True), "row", axis=0, tiled=True)
                for v in (attention_in, attention_out)
            ],
            axis=1,
        )[None]
    if aligned:
        up_blocks = lax.all_gather(expert_up[0], "col", axis=0, tiled=False)
        down_blocks = lax.all_gather(expert_down[0], "col", axis=0, tiled=False)
    else:
        up_blocks = lax.all_gather(expert_up, "col", axis=1, tiled=True)
        down_blocks = lax.all_gather(expert_down, "col", axis=2, tiled=True)

    limit = jnp.sum(
        jnp.where(
            expert_ids[:, :, None] == jnp.arange(experts, dtype=jnp.int32)[None, None, :],
            expert_capacity[None, None, :],
            0,
        ),
        axis=-1,
    )
    used = (keep_mask == 1) & (expert_slots < limit)
    slot_index = jnp.where(used, expert_ids * cap + expert_slots, -1)
    slot_cols = jnp.pad(slot_index, ((0, padded - tokens), (0, 0)), constant_values=-1)
    slot_rows = slot_cols.T
    g1 = gain_attention.reshape(1, width)
    g2 = gain_experts.reshape(1, width)
    rwt = router_weight.T

    og_out = pl.pallas_call(
        functools.partial(dispatch_kernel, blocks),
        out_shape=shape((slots, width)),
        in_specs=[VMEM, VMEM],
        out_specs=VMEM,
        scratch_shapes=[pltpu.VMEM((padded, width), BF16)],
        compiler_params=params(24),
        name="og_dispatch",
    )(output_grad, slot_rows)

    def exchange(v):
        return lax.all_to_all(v, "row", split_axis=0, concat_axis=0, tiled=True)

    og_in = exchange(og_out.reshape(experts, cap, width)).reshape(slots, width)

    proj, mixed, lse, res, probs, tok_out, sq_attn = pl.pallas_call(
        functools.partial(forward_kernel, images, experts, blocks),
        out_shape=[
            shape((padded, 3 * width)),
            shape((padded, width)),
            shape((padded, 128), F32),
            shape((padded, width), F32),
            shape((experts, padded), F32),
            shape((slots, width)),
            shape((1, width), F32),
        ],
        in_specs=[VMEM] * 6,
        out_specs=[VMEM] * 7,
        scratch_shapes=[pltpu.VMEM((padded, width), BF16)] * 4,
        compiler_params=params(48),
        cost_estimate=pl.CostEstimate(flops=6 * 10**9, bytes_accessed=90 * 10**6, transcendentals=0),
        name="attn_forward",
    )(block_input, weights, g1, g2, rwt, slot_rows)

    tok_in = exchange(tok_out.reshape(experts, cap, width)).reshape(slots, width)

    rblk = slots // blocks
    whole = lambda *dims: pl.BlockSpec(dims, lambda b: (0,) * len(dims))
    rows_spec = lambda n: pl.BlockSpec((rblk, n), lambda b: (b, 0))
    ret, gsent, hid, ginner, gr, gg_out = pl.pallas_call(
        functools.partial(expert_kernel, 512, experts // blocks, cap),
        grid=(blocks,),
        out_shape=[
            shape((slots, width)),
            shape((slots, width)),
            shape((slots, ff)),
            shape((slots, ff)),
            shape((slots, width)),
            shape((experts, cap_lanes), F32),
        ],
        in_specs=[rows_spec(width), rows_spec(width), whole(width, experts), ANY, ANY],
        out_specs=[
            rows_spec(width), rows_spec(width), rows_spec(ff), rows_spec(ff), rows_spec(width),
            whole(experts, cap_lanes),
        ],
        scratch_shapes=[
            pltpu.VMEM((width, ff), BF16),
            pltpu.VMEM((ff, width), BF16),
            pltpu.VMEM((rblk, width), F32),
            pltpu.VMEM((rblk, width), F32),
            pltpu.VMEM((cap_lanes, 128), F32),
            DMA,
            DMA,
        ],
        compiler_params=params(56),
        cost_estimate=pl.CostEstimate(flops=4 * 10**10, bytes_accessed=150 * 10**6, transcendentals=0),
        name="expert_fused",
    )(tok_in, og_in, router_weight, up_blocks, down_blocks)

    gg_all = lax.all_gather(gg_out, "row", axis=0, tiled=False)
    gg_back = lax.dynamic_index_in_dim(gg_all, lax.axis_index("row"), 1, keepdims=False)
    gback = exchange(gsent.reshape(experts, cap, width)).reshape(slots, width)
    ret, _ = lax.optimization_barrier((ret, gsent))
    back = exchange(ret.reshape(experts, cap, width)).reshape(slots, width)

    fstep = 512
    nc = ncol if aligned else 1
    up_part, down_part = pl.pallas_call(
        weight_grad_kernel,
        grid=(ff // fstep,),
        out_shape=[shape((nc, width // nc, ff)), shape((nc, ff, width // nc))],
        in_specs=[
            whole(slots, width),
            whole(slots, width),
            pl.BlockSpec((slots, fstep), lambda f: (0, f)),
            pl.BlockSpec((slots, fstep), lambda f: (0, f)),
        ],
        out_specs=[
            pl.BlockSpec((nc, width // nc, fstep), lambda f: (0, 0, f)),
            pl.BlockSpec((nc, fstep, width // nc), lambda f: (0, f, 0)),
        ],
        scratch_shapes=[pltpu.VMEM((width, slots), BF16)],
        compiler_params=params(56),
        cost_estimate=pl.CostEstimate(flops=2 * 10**10, bytes_accessed=80 * 10**6, transcendentals=0),
        name="expert_weight_grads",
    )(tok_in, gr, hid, ginner)
    if aligned:
        up_grad = lax.psum_scatter(up_part, "col", scatter_dimension=0, tiled=True).astype(F32)
        down_grad = lax.psum_scatter(down_part, "col", scatter_dimension=0, tiled=True).astype(F32)
    else:
        up_grad = lax.psum_scatter(up_part, "col", scatter_dimension=1, tiled=True).astype(F32)
        down_grad = lax.psum_scatter(down_part, "col", scatter_dimension=2, tiled=True).astype(F32)

    x_grad, wgrad, rgrad, gains = pl.pallas_call(
        functools.partial(backward_kernel, images, experts),
        out_shape=[
            shape((tokens, width)),
            shape(weights.shape),
            shape((experts, width), F32),
            shape((2, width), F32),
        ],
        in_specs=[VMEM] * 15,
        out_specs=[VMEM] * 4,
        scratch_shapes=[
            pltpu.VMEM((padded, width), BF16),
            pltpu.VMEM((padded, width), BF16),
            pltpu.VMEM((padded, slots), BF16),
            pltpu.VMEM((padded, width), F32),
            pltpu.VMEM((padded, width), F32),
            pltpu.VMEM((padded, width), BF16),
            pltpu.VMEM((padded, width), BF16),
            pltpu.VMEM((padded, 3 * width), BF16),
            pltpu.VMEM((padded, width), BF16),
            pltpu.VMEM((3 * experts, padded), BF16),
            pltpu.VMEM((128, cap_lanes), F32),
            pltpu.VMEM((16, width), F32),
        ],
        compiler_params=params(58),
        cost_estimate=pl.CostEstimate(flops=2 * 10**10, bytes_accessed=180 * 10**6, transcendentals=0),
        name="attn_backward",
    )(
        block_input, output_grad, weights, g1, g2, rwt, slot_rows, slot_cols,
        proj, mixed, lse, res, probs, gback, gg_back,
    )
    block_output, sq_moe = pl.pallas_call(
        combine_kernel,
        out_shape=[shape((tokens, width)), shape((2, width), F32)],
        in_specs=[VMEM] * 3,
        out_specs=[VMEM] * 2,
        scratch_shapes=[pltpu.VMEM((padded, slots), BF16), pltpu.VMEM((padded, width), BF16)],
        compiler_params=params(32),
        cost_estimate=pl.CostEstimate(flops=3 * 10**9, bytes_accessed=16 * 10**6, transcendentals=0),
        name="moe_combine",
    )(slot_cols, res, back)

    small = jnp.concatenate([rgrad, gains, sq_moe, sq_attn], axis=0)
    small = jnp.pad(small, ((0, -small.shape[0] % 8), (0, 0)))
    if ring:
        half = wcols // 2
        blk = lambda *lead: pltpu.VMEM(lead + (rh, wcols), BF16)
        hblk = lambda *lead: pltpu.VMEM(lead + (rh, half), BF16)
        merged, small = pl.pallas_call(
            reduce_kernel,
            out_shape=[shape((rh, wcols), F32), shape(small.shape, F32)],
            in_specs=[VMEM] * 2,
            out_specs=[VMEM] * 2,
            scratch_shapes=[
                blk(4, 2, 2), blk(4, 2, 2), hblk(4, 2), hblk(4, 2), hblk(4), hblk(4), blk(3),
                pltpu.VMEM((5,) + small.shape, F32), pltpu.VMEM((5,) + small.shape, F32),
                DMA((16,)), DMA((16,)), DMA((8,)), DMA((8,)), DMA((8,)), DMA((8,)),
                DMA((3,)), DMA((3,)), DMA((5,)), DMA((5,)),
            ],
            compiler_params=params(40, collective_id=1, has_side_effects=True),
            name="attn_grads_reduce",
        )(wgrad, small)
        in_grad = merged[:, : 3 * width // ncol]
        out_grad = merged[:, 3 * width // ncol :]
    else:
        merged = lax.psum_scatter(wgrad[0], "row", scatter_dimension=0, tiled=True)
        in_grad = lax.psum_scatter(
            merged[:, : 3 * width], "col", scatter_dimension=1, tiled=True
        ).astype(F32)
        out_grad = lax.psum_scatter(
            merged[:, 3 * width :], "col", scatter_dimension=1, tiled=True
        ).astype(F32)
        small = lax.psum(small, ("row", "col"))
    rgrad = small[:experts]
    gains = small[experts : experts + 2]
    sums = jnp.sum(small[experts + 2 : experts + 5], axis=1)
    squares = jnp.stack([sums[0], sums[2], sums[1]])
    residual_rms = jnp.sqrt(squares / (tokens * nrow * ncol * width))
    return (
        block_output, x_grad, in_grad, out_grad,
        up_grad.reshape(1, width // ncol, ff), down_grad.reshape(1, ff, width // ncol),
        rgrad.T, gains[0], gains[1], residual_rms,
    )


def solution(mesh):
    tok = P(("row", "col"), None)
    grid = P("row", "col")
    up, down = P("row", "col", None), P("row", None, "col")
    return jax.shard_map(
        per_device,
        mesh=mesh,
        in_specs=(tok, grid, grid, up, down, P(), P(), P(), tok, tok, P(), tok, tok),
        out_specs=(tok, tok, grid, grid, up, down, P(), P(), P(), P()),
        check_vma=False,
    )
```
